256 devices in a mesh: seq: 64 (over z, x, core), head: 4 (over y).
Axes of the slice: x: 4, y: 4, z: 8, core: 2. Of those that a mesh axis runs over, the one named last changes fastest.
Arguments:
- queries: bfloat16 [2048, 2560], P('seq', 'head'), may hold values from -24 to 24
- new_keys: bfloat16 [2048, 2560], P('seq', 'head'), may hold values from -7 to 7
- new_values: bfloat16 [2048, 2560], P('seq', 'head'), may hold values from -6 to 6
- key_cache: bfloat16 [8192, 2560], P('seq', 'head'), may hold values from -7 to 7
- value_cache: bfloat16 [8192, 2560], P('seq', 'head'), may hold values from -6 to 6
- out_weight: bfloat16 [2560, 5120], P('head'), may hold values from -0.125 to 0.125
- gate: float32 [5120], P('head'), may hold values from 0.4 to 1.6
- refresh_index: int32 [64, 32], P('seq'), may hold values from 0 to 127, as said below
- refresh_count: int32 [64], P('seq'), may hold values from 1 to 32, 1024 in all
Outputs:
- update: bfloat16 [2048, 5120], P('seq', 'head')
The draws below stay inside these ranges and needn't reach their ends.
Inputs may be any that keep to these rules, and one draw needn't show every extreme that they name: `refresh_index`: each row holds 32 distinct token positions of that seq index; only the first refresh_count of them are used. `refresh_count`: the counts sum to 16 times the number of seq indices.
All inputs are finite; a program needn't handle non-finite values. No bound on the sum of `refresh_count` on one device may be relied on, other than what follows from the above.
Results may differ from the reference program's by a relative error of at most 0.015.
Values may be sent and summed in bfloat16 or wider, within the bound.
A program may use at most 64 MiB of HBM per device.

```python
import math
import jax
import jax.numpy as jnp
import numpy as np
from jax import lax

D = 5120
HEADS = 20
HD = 128
TOK_DEV = 128
REF_MOST = 32
REF_BAL = 16
SLOTS = 2048
TOKENS = 8192
N_SEQ = 64


def pair_draw(key):
    row_width = HEADS * HD
    key_query = jax.random.fold_in(key, 11)
    key_keys = jax.random.fold_in(key, 12)
    query_rows = jnp.clip(1.7 * jax.random.normal(key_query, (SLOTS, row_width), jnp.float32), -7.0, 7.0)
    key_rows = jnp.clip(1.7 * jax.random.normal(key_keys, (SLOTS, row_width), jnp.float32), -7.0, 7.0)
    return (query_rows.astype(jnp.bfloat16), key_rows.astype(jnp.bfloat16))


def draw_queries(key, part):
    return pair_draw(key)[0]


def draw_new_keys(key, part):
    return pair_draw(key)[1]


def draw_refresh_index(key, part):
    seq_count = SLOTS // REF_MOST
    ranks = jax.random.randint(key, (seq_count, TOK_DEV), 0, 1 << 20, jnp.int32)
    ranks = ranks * TOK_DEV + jnp.arange(TOK_DEV, dtype=jnp.int32)[None, :]
    ranks = ranks.at[0, TOK_DEV - 1].set(-2)
    ranks = ranks.at[0, 0].set(-1)
    order = jnp.argsort(ranks, axis=1, stable=True)
    return order[:, :REF_MOST].astype(jnp.int32)


def steps_of(key, shape, split, low, top_value):
    def one(axis_at, shards_of):
        heights = jax.random.uniform(jax.random.fold_in(jax.random.fold_in(key, 6), axis_at), (shards_of,), jnp.float32, low / len(split), top_value / len(split))
        return jnp.repeat(jnp.exp(heights), shape[axis_at] // shards_of).reshape((-1,) + (1,) * (len(shape) - axis_at - 1))

    factor_of = one(*split[0])
    for cut in split[1:]:
        factor_of = factor_of * one(*cut)
    return factor_of


def split_up(count, total, bound, slope):
    loads = [(1 << 20) // math.isqrt(grade ** slope) + 1 for grade in range(2, count + 1)]
    rest, counts = total - bound - (count - 1), [1] * (count - 1)
    while rest > 0:
        candidates = [i for i in range(count - 1) if counts[i] < bound]
        pool, remaining = sum([loads[i] for i in candidates]), rest
        for i in candidates:
            addition = min(bound - counts[i], max(1, remaining * loads[i] // pool), rest)
            counts[i] = counts[i] + addition
            rest = rest - addition
    return np.array([bound] + counts)


def ragged(stream_key, amount, total, limit, lean):
    if amount == 2:
        one = jax.random.randint(stream_key, (), max(1, total - limit), min(limit, total - 1) + 1)
        return jnp.stack([one, total - one])
    tallies = jnp.asarray(split_up(amount, total, limit, lean), jnp.int32)
    couples = (amount - 1) // 2
    giver, taker = tallies[1:1 + 2 * couples:2], tallies[2:2 + 2 * couples:2]
    room = jnp.minimum(giver - 1, limit - taker)
    moved = jax.random.randint(jax.random.fold_in(stream_key, 1), (couples,), 0, 1 << 20) % (room + 1)
    tallies = tallies.at[1:1 + 2 * couples:2].set(giver - moved).at[2:2 + 2 * couples:2].set(taker + moved)
    return tallies[jax.random.permutation(jax.random.fold_in(stream_key, 2), amount)]


def bell_draw(key, dims, width, bound, pieces=(), kind=jnp.bfloat16):
    factor_of = steps_of(key, dims, pieces, -0.22, 0.18) if pieces else 1.0
    result = jax.random.normal(key, dims, jnp.float32) * width * factor_of
    return jnp.minimum(jnp.maximum(result, -bound), bound).astype(kind)


def setup_inputs(seed: int = 0) -> dict:
    streams_of = jax.random.split(jax.random.key(seed), 10)
    return {
        "queries": draw_queries(jax.random.fold_in(streams_of[9], 71), 0),
        "new_keys": draw_new_keys(jax.random.fold_in(streams_of[9], 71), 0),
        "new_values": bell_draw(streams_of[2], (SLOTS, HEADS * HD), 1.0, 6.0, ((0, 64), (1, 4))),
        "key_cache": bell_draw(streams_of[3], (TOKENS, HEADS * HD), 1.7, 7.0, ((0, 64), (1, 4))),
        "value_cache": bell_draw(streams_of[4], (TOKENS, HEADS * HD), 1.0, 6.0, ((0, 64), (1, 4))),
        "out_weight": bell_draw(streams_of[5], (HEADS * HD, D), (HEADS * HD) ** -0.5, 0.125, ((0, 4),)),
        "gate": jnp.clip(0.4 + 1.2 * jax.random.uniform(streams_of[6], (D,), jnp.float32) ** steps_of(streams_of[6], (D,), ((0, 4),), -0.2, 0.2), 0.4, 1.6),
        "refresh_index": draw_refresh_index(jax.random.fold_in(streams_of[9], 71), 0),
        "refresh_count": ragged(streams_of[8], N_SEQ, REF_BAL * N_SEQ, REF_MOST, 2).astype(jnp.int32),
    }


def head_attention(inputs):
    q_head, k_head, v_head = inputs
    scores = jnp.dot(q_head, k_head.T, preferred_element_type=jnp.float32) * (HD ** -0.5)
    row_top = jnp.max(scores, axis=1, keepdims=True)
    weights = jnp.exp(scores - row_top)
    row_total = jnp.sum(weights, axis=1, keepdims=True)
    summed = jnp.dot(weights.astype(jnp.bfloat16), v_head, preferred_element_type=jnp.float32)
    return summed / row_total


def reference(queries, new_keys, new_values, key_cache, value_cache, out_weight, gate, refresh_index, refresh_count):
    seq_count = refresh_count.shape[0]
    live_slots = jnp.arange(REF_MOST)[None, :] < refresh_count[:, None]
    targets = refresh_index.astype(jnp.int32) + (jnp.arange(seq_count) * TOK_DEV).astype(jnp.int32)[:, None]
    targets = jnp.where(live_slots, targets, TOKENS).reshape(-1).astype(jnp.int32)
    keys = key_cache.at[targets].set(new_keys, mode="drop")
    values = value_cache.at[targets].set(new_values, mode="drop")
    q_heads = queries.reshape(SLOTS, HEADS, HD).transpose(1, 0, 2)
    k_heads = keys.reshape(TOKENS, HEADS, HD).transpose(1, 0, 2)
    v_heads = values.reshape(TOKENS, HEADS, HD).transpose(1, 0, 2)
    attended = lax.map(head_attention, (q_heads, k_heads, v_heads))
    attended = attended.transpose(1, 0, 2).reshape(SLOTS, HEADS * HD).astype(jnp.bfloat16)
    projected = jnp.dot(attended, out_weight, preferred_element_type=jnp.float32)
    live_rows = live_slots.reshape(-1).astype(jnp.float32)[:, None]
    return (gate[None, :] * projected * live_rows).astype(jnp.bfloat16)
```

```python
import functools
import math

import jax
import jax.numpy as jnp
from jax import lax
from jax.experimental import pallas as pl
from jax.experimental.pallas import tpu as pltpu
from jax.sharding import PartitionSpec as P

HD = 128
X = 4
CORES = 2
MESH = pl.DeviceIdType.MESH


def kernel(
    rings,
    q_hbm,
    new_k_hbm,
    new_v_hbm,
    cache_k_hbm,
    cache_v_hbm,
    weight_hbm,
    gate_ref,
    index_ref,
    count_ref,
    out_ref,
    cache,
    fresh,
    q_buf,
    kv_buf,
    o_send,
    o_recv,
    stat_send,
    stat_recv,
    weight,
    proj,
    y_send,
    y_recv,
    local_sem,
    q_ssem,
    q_rsem,
    own_ssem,
    own_rsem,
    relay_ssem,
    relay_rsem,
    pair_ssem,
    pair_rsem,
    o_ssem,
    o_rsem,
    stat_ssem,
    stat_rsem,
    y_ssem,
    y_rsem,
):
    depth, width = rings
    heads = q_buf.shape[0]
    slots = q_buf.shape[2]
    tokens = kv_buf.shape[3]
    out_cols = out_ref.shape[1]
    groups = stat_send.shape[1]
    per_group = depth // groups
    factor = HD ** (-0.5) * math.log2(math.e)

    me = lax.axis_index("seq")
    y = lax.axis_index("head")
    z = me // (X * CORES)
    x = (me // CORES) % X
    core = me % CORES

    def at_seq(z_at, x_at, core_at):
        return {"seq": (z_at * X + x_at) * CORES + core_at, "head": y}

    def z_peer(step):
        return at_seq((z + step) % depth, x, core)

    def y_peer(step):
        return {"seq": me, "head": (y + step) % width}

    right = at_seq(z, (x + 1) % X, core)
    left = at_seq(z, (x + X - 1) % X, core)
    sibling = at_seq(z, x, 1 - core)

    def remote(src, dst, send, recv, device):
        return pltpu.make_async_remote_copy(
            src_ref=src,
            dst_ref=dst,
            send_sem=send,
            recv_sem=recv,
            device_id=device,
            device_id_type=MESH,
        )

    barrier = pltpu.get_barrier_semaphore()
    peers = (
        [z_peer(step) for step in range(1, depth)]
        + [y_peer(step) for step in range(1, width)]
        + [right, left, sibling]
    )
    for peer in peers:
        pl.semaphore_signal(barrier, inc=1, device_id=peer, device_id_type=MESH)

    loads = [
        pltpu.make_async_copy(cache_k_hbm, cache.at[0], local_sem.at[0]),
        pltpu.make_async_copy(cache_v_hbm, cache.at[1], local_sem.at[1]),
        pltpu.make_async_copy(new_k_hbm, fresh.at[0], local_sem.at[2]),
        pltpu.make_async_copy(new_v_hbm, fresh.at[1], local_sem.at[3]),
    ]
    q_loads = [
        pltpu.make_async_copy(
            q_hbm.at[:, pl.ds(h * HD, HD)], q_buf.at[h, 0], local_sem.at[5 + h]
        )
        for h in range(heads)
    ]
    weight_load = pltpu.make_async_copy(weight_hbm, weight, local_sem.at[4])
    for load in loads + q_loads + [weight_load]:
        load.start()

    matches = (
        lax.broadcasted_iota(jnp.int32, (tokens, slots), 0) == index_ref[...]
    ) & (lax.broadcasted_iota(jnp.int32, (tokens, slots), 1) < count_ref[...])
    chosen = matches.astype(jnp.float32)
    replaced = jnp.max(chosen, axis=1, keepdims=True) > 0.5
    chosen = chosen.astype(jnp.bfloat16)
    for load in loads:
        load.wait()
    for part in range(2):
        placed = jnp.dot(chosen, fresh[part], preferred_element_type=jnp.float32)
        for h in range(heads):
            cols = slice(h * HD, (h + 1) * HD)
            kv_buf[h, part, 0] = jnp.where(
                replaced, placed[:, cols], cache[part, :, cols].astype(jnp.float32)
            ).astype(jnp.bfloat16)
    for load in q_loads:
        load.wait()

    pl.semaphore_wait(barrier, len(peers))

    def own_copies(h):
        src = kv_buf.at[h, :, 0]
        return (
            remote(src, kv_buf.at[h, :, 1], own_ssem.at[h, 0], own_rsem.at[h, 0], right),
            remote(src, kv_buf.at[h, :, 2], own_ssem.at[h, 1], own_rsem.at[h, 1], left),
        )

    def relay_copies(h):
        return (
            remote(
                kv_buf.at[h, 0, 1], kv_buf.at[h, 0, 3], relay_ssem.at[h, 0], relay_rsem.at[h, 0], right
            ),
            remote(
                kv_buf.at[h, 1, 2], kv_buf.at[h, 1, 3], relay_ssem.at[h, 1], relay_rsem.at[h, 1], left
            ),
        )

    def pair_copy(h, which):
        first, count = ((0, 1), (1, 2), (3, 1))[which]
        return remote(
            kv_buf.at[h, :, pl.ds(first, count)],
            kv_buf.at[h, :, pl.ds(X + first, count)],
            pair_ssem.at[h, which],
            pair_rsem.at[h, which],
            sibling,
        )

    def q_copy(h, step):
        return remote(
            q_buf.at[h, 0], q_buf.at[h, step], q_ssem.at[h, step], q_rsem.at[h, step], z_peer(step)
        )

    def o_copy(h, step):
        return remote(
            o_send.at[h, step],
            o_recv.at[h, step],
            o_ssem.at[h, step],
            o_rsem.at[h, step],
            z_peer(depth - step),
        )

    def stat_copy(h, step):
        return remote(
            stat_send.at[h, step // per_group],
            stat_recv.at[h, step],
            stat_ssem.at[h, step],
            stat_rsem.at[h, step],
            z_peer(depth - step),
        )

    far_first = sorted(range(1, depth), key=lambda step: -min(step, depth - step))

    def each_head(body):
        lax.fori_loop(0, heads, lambda h, carry: (body(h), carry)[1], 0)

    for h in range(min(2, heads)):
        for copy in own_copies(h):
            copy.start()
        pair_copy(h, 0).start()

    def send_queries(h):
        for step in far_first:
            q_copy(h, step).start()

    each_head(send_queries)

    lane = lax.broadcasted_iota(jnp.int32, (per_group * slots, HD), 1)
    row = lax.broadcasted_iota(jnp.int32, (per_group * slots, HD), 0)
    diagonal = lane == row

    def to_row(column):
        spread = jnp.broadcast_to(column, (per_group * slots, HD))
        return jnp.sum(jnp.where(diagonal, spread, 0.0), axis=0, keepdims=True)

    def attend(h):
        queries = q_buf[h].reshape(depth * slots, HD)
        keys = kv_buf[h, 0].reshape(X * CORES * tokens, HD)
        values = kv_buf[h, 1].reshape(X * CORES * tokens, HD)
        scores = (
            lax.dot_general(
                queries, keys, (((1,), (1,)), ((), ())), preferred_element_type=jnp.float32
            )
            * factor
        )
        top = jnp.max(scores, axis=1, keepdims=True)
        weights = jnp.exp2(scores - top)
        total = jnp.sum(weights, axis=1, keepdims=True)
        summed = jnp.dot(
            weights.astype(jnp.bfloat16), values, preferred_element_type=jnp.float32
        ).astype(jnp.bfloat16)
        o_send[h] = summed.reshape(depth, slots, HD)
        o_recv[h, 0] = summed[:slots]
        for g in range(groups):
            rows = slice(g * per_group * slots, (g + 1) * per_group * slots)
            top_row, total_row = to_row(top[rows]), to_row(total[rows])
            stat_send[h, g, 0] = top_row
            stat_send[h, g, 1] = total_row
            if g == 0:
                stat_recv[h, 0, 0] = top_row
                stat_recv[h, 0, 1] = total_row

    def stage(step, carry):
        @pl.when(step < heads)
        def _():
            for copy in own_copies(step):
                copy.wait_recv()
            for copy in relay_copies(step):
                copy.start()
            pair_copy(step, 1).start()

            @pl.when(step + 2 < heads)
            def _():
                for copy in own_copies(step + 2):
                    copy.start()
                pair_copy(step + 2, 0).start()

        @pl.when(step >= 1)
        def _():
            h = step - 1
            for copy in relay_copies(h):
                copy.wait_recv()
            pair_copy(h, 2).start()
            for ring in range(1, depth):
                q_copy(h, ring).wait_recv()
            for which in range(3):
                pair_copy(h, which).wait_recv()
            attend(h)
            for ring in far_first:
                o_copy(h, ring).start()
                stat_copy(h, ring).start()

        return carry

    lax.fori_loop(0, heads + 1, stage, 0)

    weight_load.wait()
    lane_row = lax.broadcasted_iota(jnp.int32, (1, HD), 1) // slots
    lanes = depth * slots
    spot = lax.broadcasted_iota(jnp.int32, (slots, lanes), 1) % slots
    on_row = spot == lax.broadcasted_iota(jnp.int32, (slots, lanes), 0)

    def over_lanes(rows, op):
        folded = functools.reduce(op, rows)
        shift = slots
        while shift < HD:
            folded = op(folded, pltpu.roll(folded, shift, 1))
            shift *= 2
        return folded

    def combined(h):
        for step in range(1, depth):
            o_copy(h, step).wait_recv()
            stat_copy(h, step).wait_recv()
        tops, totals = [], []
        for g in range(groups):
            top_row, total_row = (stat_recv[h, g * per_group, 0], stat_recv[h, g * per_group, 1])
            for k in range(1, per_group):
                here = lane_row == k
                top_row = jnp.where(here, stat_recv[h, g * per_group + k, 0], top_row)
                total_row = jnp.where(here, stat_recv[h, g * per_group + k, 1], total_row)
            tops.append(top_row)
            totals.append(total_row)
        peak = over_lanes(tops, jnp.maximum)
        shares = [jnp.exp2(top_row - peak) for top_row in tops]
        whole = over_lanes([share * total for share, total in zip(shares, totals)], jnp.add)
        factors = jnp.concatenate([share / whole for share in shares], axis=1)
        spread = jnp.where(on_row, jnp.broadcast_to(factors, (slots, lanes)), 0.0)
        high = spread.astype(jnp.bfloat16)
        low = (spread - high.astype(jnp.float32)).astype(jnp.bfloat16)
        parts = o_recv[h].reshape(lanes, HD)
        return (
            jnp.dot(high, parts, preferred_element_type=jnp.float32)
            + jnp.dot(low, parts, preferred_element_type=jnp.float32)
        ).astype(jnp.bfloat16)

    def projected(attended, h, step):
        start = pl.multiple_of(((y + step) % width) * out_cols, HD)
        block = weight[pl.ds(pl.multiple_of(h * HD, HD), HD), pl.ds(start, out_cols)]
        return jnp.dot(attended, block, preferred_element_type=jnp.float32)

    proj[...] = jnp.zeros_like(proj)

    def project(h, carry):
        attended = combined(h)
        for step in range(width):
            proj[step] += projected(attended, h, step)
        return carry

    lax.fori_loop(0, heads - 1, project, 0)

    def y_copy(step):
        return remote(
            y_send.at[step - 1], y_recv.at[step - 1], y_ssem.at[step - 1], y_rsem.at[step - 1], y_peer(step)
        )

    attended = combined(heads - 1)
    for step in sorted(range(1, width), key=lambda step: -min(step, width - step)):
        y_send[step - 1] = (proj[step] + projected(attended, heads - 1, step)).astype(jnp.bfloat16)
        y_copy(step).start()
    result = proj[0] + projected(attended, heads - 1, 0)
    for step in range(1, width):
        y_copy(step).wait_recv()
        result += y_recv[step - 1].astype(jnp.float32)
    live = lax.broadcasted_iota(jnp.int32, (slots, out_cols), 0) < count_ref[...]
    out_ref[...] = (
        gate_ref[...] * result * live.astype(jnp.float32)
    ).astype(jnp.bfloat16)

    def drain(h):
        for copy in own_copies(h) + relay_copies(h):
            copy.wait_send()
        for which in range(3):
            pair_copy(h, which).wait_send()
        for step in range(1, depth):
            q_copy(h, step).wait_send()
            o_copy(h, step).wait_send()
            stat_copy(h, step).wait_send()

    each_head(drain)
    for step in range(1, width):
        y_copy(step).wait_send()


def on_device(
    depth,
    width,
    queries,
    new_keys,
    new_values,
    key_cache,
    value_cache,
    out_weight,
    gate,
    refresh_index,
    refresh_count,
):
    slots, row_width = queries.shape
    tokens = key_cache.shape[0]
    heads = row_width // HD
    out_cols = gate.shape[0]
    groups = max(1, depth * slots // HD)
    bf16, f32 = jnp.bfloat16, jnp.float32
    dma = pltpu.SemaphoreType.DMA
    any_spec = pl.BlockSpec(memory_space=pl.ANY)
    vmem_spec = pl.BlockSpec(memory_space=pltpu.VMEM)
    return pl.pallas_call(
        functools.partial(kernel, (depth, width)),
        out_shape=jax.ShapeDtypeStruct((slots, out_cols), bf16),
        in_specs=[any_spec] * 6 + [vmem_spec] * 3,
        out_specs=vmem_spec,
        scratch_shapes=[
            pltpu.VMEM((2, tokens, row_width), bf16),
            pltpu.VMEM((2, slots, row_width), bf16),
            pltpu.VMEM((heads, depth, slots, HD), bf16),
            pltpu.VMEM((heads, 2, X * CORES, tokens, HD), bf16),
            pltpu.VMEM((heads, depth, slots, HD), bf16),
            pltpu.VMEM((heads, depth, slots, HD), bf16),
            pltpu.VMEM((heads, groups, 2, 1, HD), f32),
            pltpu.VMEM((heads, depth, 2, 1, HD), f32),
            pltpu.VMEM(out_weight.shape, bf16),
            pltpu.VMEM((width, slots, out_cols), f32),
            pltpu.VMEM((max(1, width - 1), slots, out_cols), bf16),
            pltpu.VMEM((max(1, width - 1), slots, out_cols), bf16),
            dma((5 + heads,)),
            dma((heads, depth)),
            dma((heads, depth)),
            dma((heads, 2)),
            dma((heads, 2)),
            dma((heads, 2)),
            dma((heads, 2)),
            dma((heads, 3)),
            dma((heads, 3)),
            dma((heads, depth)),
            dma((heads, depth)),
            dma((heads, depth)),
            dma((heads, depth)),
            dma((max(1, width - 1),)),
            dma((max(1, width - 1),)),
        ],
        compiler_params=pltpu.CompilerParams(
            collective_id=0, has_side_effects=True, vmem_limit_bytes=40 << 20
        ),
    )(
        queries,
        new_keys,
        new_values,
        key_cache,
        value_cache,
        out_weight,
        gate.reshape(1, -1),
        refresh_index,
        refresh_count.reshape(1, 1),
    )


def solution(mesh):
    depth = mesh.shape["seq"] // (X * CORES)
    width = mesh.shape["head"]
    return jax.shard_map(
        functools.partial(on_device, depth, width),
        mesh=mesh,
        in_specs=(
            P("seq", "head"),
            P("seq", "head"),
            P("seq", "head"),
            P("seq", "head"),
            P("seq", "head"),
            P("head", None),
            P("head"),
            P("seq", None),
            P("seq"),
        ),
        out_specs=P("seq", "head"),
        check_vma=False,
    )
```

```python
import functools
import math

import jax
import jax.numpy as jnp
from jax import lax
from jax.experimental import pallas as pl
from jax.experimental.pallas import tpu as pltpu
from jax.sharding import PartitionSpec as P

HD = 128
X = 4
CORES = 2
MESH = pl.DeviceIdType.MESH
AHEAD = 3
LAG = 2


def kernel(
    rings,
    q_hbm,
    new_k_hbm,
    new_v_hbm,
    cache_k_hbm,
    cache_v_hbm,
    weight_hbm,
    index_ref,
    count_ref,
    out_ref,
    cache,
    fresh,
    q_buf,
    kv_buf,
    o_send,
    o_recv,
    stat_send,
    stat_recv,
    weight,
    proj,
    y_send,
    y_recv,
    local_sem,
    q_ssem,
    q_rsem,
    own_ssem,
    own_rsem,
    relay_ssem,
    relay_rsem,
    pair_ssem,
    pair_rsem,
    o_ssem,
    o_rsem,
    stat_ssem,
    stat_rsem,
    y_ssem,
    y_rsem,
):
    depth, width = rings
    heads = q_buf.shape[0]
    slots = q_buf.shape[2]
    tokens = kv_buf.shape[3]
    out_cols = out_ref.shape[1]
    groups = stat_send.shape[1]
    per_group = depth // groups
    factor = HD ** (-0.5) * math.log2(math.e)

    me = lax.axis_index("seq")
    y = lax.axis_index("head")
    z = me // (X * CORES)
    x = (me // CORES) % X
    core = me % CORES

    def at_seq(z_at, x_at, core_at):
        return {"seq": (z_at * X + x_at) * CORES + core_at, "head": y}

    def z_peer(step):
        return at_seq((z + step) % depth, x, core)

    def y_peer(step):
        return {"seq": me, "head": (y + step) % width}

    right = at_seq(z, (x + 1) % X, core)
    left = at_seq(z, (x + X - 1) % X, core)
    sibling = at_seq(z, x, 1 - core)

    def remote(src, dst, send, recv, device):
        return pltpu.make_async_remote_copy(
            src_ref=src,
            dst_ref=dst,
            send_sem=send,
            recv_sem=recv,
            device_id=device,
            device_id_type=MESH,
        )

    barrier = pltpu.get_barrier_semaphore()
    peers = (
        [z_peer(step) for step in range(1, depth)]
        + [y_peer(step) for step in range(1, width)]
        + [right, left, sibling]
    )
    for peer in peers:
        pl.semaphore_signal(barrier, inc=1, device_id=peer, device_id_type=MESH)

    loads = [
        pltpu.make_async_copy(cache_k_hbm, cache.at[0], local_sem.at[0]),
        pltpu.make_async_copy(cache_v_hbm, cache.at[1], local_sem.at[1]),
        pltpu.make_async_copy(new_k_hbm, fresh.at[0], local_sem.at[2]),
        pltpu.make_async_copy(new_v_hbm, fresh.at[1], local_sem.at[3]),
    ]
    q_loads = [
        pltpu.make_async_copy(
            q_hbm.at[:, pl.ds(h * HD, HD)], q_buf.at[h, 0], local_sem.at[5 + h]
        )
        for h in range(heads)
    ]
    weight_load = pltpu.make_async_copy(weight_hbm, weight, local_sem.at[4])
    for load in loads + q_loads + [weight_load]:
        load.start()

    matches = (
        lax.broadcasted_iota(jnp.int32, (tokens, slots), 0) == index_ref[...]
    ) & (lax.broadcasted_iota(jnp.int32, (tokens, slots), 1) < count_ref[...])
    chosen = matches.astype(jnp.float32)
    replaced = jnp.max(chosen, axis=1, keepdims=True) > 0.5
    chosen = chosen.astype(jnp.bfloat16)
    for load in loads:
        load.wait()
    for part in range(2):
        placed = jnp.dot(chosen, fresh[part], preferred_element_type=jnp.float32)
        for h in range(heads):
            cols = slice(h * HD, (h + 1) * HD)
            kv_buf[h, part, 0] = jnp.where(
                replaced, placed[:, cols], cache[part, :, cols].astype(jnp.float32)
            ).astype(jnp.bfloat16)
    for load in q_loads:
        load.wait()

    pl.semaphore_wait(barrier, len(peers))

    def own_copies(h):
        src = kv_buf.at[h, :, 0]
        return (
            remote(src, kv_buf.at[h, :, 1], own_ssem.at[h, 0], own_rsem.at[h, 0], right),
            remote(src, kv_buf.at[h, :, 2], own_ssem.at[h, 1], own_rsem.at[h, 1], left),
        )

    def relay_copies(h):
        return (
            remote(
                kv_buf.at[h, 0, 1], kv_buf.at[h, 0, 3], relay_ssem.at[h, 0], relay_rsem.at[h, 0], right
            ),
            remote(
                kv_buf.at[h, 1, 2], kv_buf.at[h, 1, 3], relay_ssem.at[h, 1], relay_rsem.at[h, 1], left
            ),
        )

    def pair_copy(h, which):
        first, count = ((0, 1), (1, 2), (3, 1))[which]
        return remote(
            kv_buf.at[h, :, pl.ds(first, count)],
            kv_buf.at[h, :, pl.ds(X + first, count)],
            pair_ssem.at[h, which],
            pair_rsem.at[h, which],
            sibling,
        )

    def q_copy(h, step):
        return remote(
            q_buf.at[h, 0], q_buf.at[h, step], q_ssem.at[h, step], q_rsem.at[h, step], z_peer(step)
        )

    def o_copy(h, step):
        return remote(
            o_send.at[h, step],
            o_recv.at[h, step],
            o_ssem.at[h, step],
            o_rsem.at[h, step],
            z_peer(depth - step),
        )

    def stat_copy(h, step):
        return remote(
            stat_send.at[h, step // per_group],
            stat_recv.at[h, step],
            stat_ssem.at[h, step],
            stat_rsem.at[h, step],
            z_peer(depth - step),
        )

    far_first = sorted(range(1, depth), key=lambda step: -min(step, depth - step))

    def each_head(body):
        lax.fori_loop(0, heads, lambda h, carry: (body(h), carry)[1], 0)

    for h in range(min(AHEAD, heads)):
        for copy in own_copies(h):
            copy.start()
        pair_copy(h, 0).start()

    def send_queries(h):
        for step in far_first:
            q_copy(h, step).start()

    each_head(send_queries)

    lane = lax.broadcasted_iota(jnp.int32, (per_group * slots, HD), 1)
    row = lax.broadcasted_iota(jnp.int32, (per_group * slots, HD), 0)
    diagonal = lane == row

    def to_row(column):
        spread = jnp.broadcast_to(column, (per_group * slots, HD))
        return jnp.sum(jnp.where(diagonal, spread, 0.0), axis=0, keepdims=True)

    def attend(h):
        queries = q_buf[h].reshape(depth * slots, HD)
        keys = kv_buf[h, 0].reshape(X * CORES * tokens, HD)
        values = kv_buf[h, 1].reshape(X * CORES * tokens, HD)
        scores = (
            lax.dot_general(
                queries, keys, (((1,), (1,)), ((), ())), preferred_element_type=jnp.float32
            )
            * factor
        )
        top = jnp.max(scores, axis=1, keepdims=True)
        weights = jnp.exp2(scores - top)
        total = jnp.sum(weights, axis=1, keepdims=True)
        summed = jnp.dot(
            weights.astype(jnp.bfloat16), values, preferred_element_type=jnp.float32
        ).astype(jnp.bfloat16)
        o_send[h] = summed.reshape(depth, slots, HD)
        o_recv[h, 0] = summed[:slots]
        for g in range(groups):
            rows = slice(g * per_group * slots, (g + 1) * per_group * slots)
            top_row, total_row = to_row(top[rows]), to_row(total[rows])
            stat_send[h, g, 0] = top_row
            stat_send[h, g, 1] = total_row
            if g == 0:
                stat_recv[h, 0, 0] = top_row
                stat_recv[h, 0, 1] = total_row

    def stage(step, carry):
        @pl.when(step < heads)
        def _():
            for copy in own_copies(step):
                copy.wait_recv()
            for copy in relay_copies(step):
                copy.start()
            pair_copy(step, 1).start()

            @pl.when(step + AHEAD < heads)
            def _():
                for copy in own_copies(step + AHEAD):
                    copy.start()
                pair_copy(step + AHEAD, 0).start()

        @pl.when((step >= 1) & (step <= heads))
        def _():
            h = step - 1
            for copy in relay_copies(h):
                copy.wait_recv()
            pair_copy(h, 2).start()

        @pl.when(step >= LAG)
        def _():
            h = step - LAG
            for ring in range(1, depth):
                q_copy(h, ring).wait_recv()
            for which in range(3):
                pair_copy(h, which).wait_recv()
            attend(h)
            for ring in far_first:
                o_copy(h, ring).start()
                stat_copy(h, ring).start()

        return carry

    lax.fori_loop(0, heads + LAG, stage, 0)

    weight_load.wait()
    lane_row = lax.broadcasted_iota(jnp.int32, (1, HD), 1) // slots
    lanes = depth * slots
    spot = lax.broadcasted_iota(jnp.int32, (slots, lanes), 1) % slots
    on_row = spot == lax.broadcasted_iota(jnp.int32, (slots, lanes), 0)

    def over_lanes(rows, op):
        folded = functools.reduce(op, rows)
        shift = slots
        while shift < HD:
            folded = op(folded, pltpu.roll(folded, shift, 1))
            shift *= 2
        return folded

    def combined(h):
        for step in range(1, depth):
            o_copy(h, step).wait_recv()
            stat_copy(h, step).wait_recv()
        tops, totals = [], []
        for g in range(groups):
            top_row, total_row = (stat_recv[h, g * per_group, 0], stat_recv[h, g * per_group, 1])
            for k in range(1, per_group):
                here = lane_row == k
                top_row = jnp.where(here, stat_recv[h, g * per_group + k, 0], top_row)
                total_row = jnp.where(here, stat_recv[h, g * per_group + k, 1], total_row)
            tops.append(top_row)
            totals.append(total_row)
        peak = over_lanes(tops, jnp.maximum)
        shares = [jnp.exp2(top_row - peak) for top_row in tops]
        whole = over_lanes([share * total for share, total in zip(shares, totals)], jnp.add)
        factors = jnp.concatenate([share / whole for share in shares], axis=1)
        spread = jnp.where(on_row, jnp.broadcast_to(factors, (slots, lanes)), 0.0)
        high = spread.astype(jnp.bfloat16)
        low = (spread - high.astype(jnp.float32)).astype(jnp.bfloat16)
        parts = o_recv[h].reshape(lanes, HD)
        return (
            jnp.dot(high, parts, preferred_element_type=jnp.float32)
            + jnp.dot(low, parts, preferred_element_type=jnp.float32)
        ).astype(jnp.bfloat16)

    def projected(attended, h, step):
        start = pl.multiple_of(((y + step) % width) * out_cols, HD)
        block = weight[pl.ds(pl.multiple_of(h * HD, HD), HD), pl.ds(start, out_cols)]
        return jnp.dot(attended, block, preferred_element_type=jnp.float32)

    proj[...] = jnp.zeros_like(proj)

    def project(h, carry):
        attended = combined(h)
        for step in range(width):
            proj[step] += projected(attended, h, step)
        return carry

    lax.fori_loop(0, heads - 1, project, 0)

    def y_copy(step):
        return remote(
            y_send.at[step - 1], y_recv.at[step - 1], y_ssem.at[step - 1], y_rsem.at[step - 1], y_peer(step)
        )

    attended = combined(heads - 1)
    for step in sorted(range(1, width), key=lambda step: -min(step, width - step)):
        y_send[step - 1] = (proj[step] + projected(attended, heads - 1, step)).astype(jnp.bfloat16)
        y_copy(step).start()
    result = proj[0] + projected(attended, heads - 1, 0)
    for step in range(1, width):
        y_copy(step).wait_recv()
        result += y_recv[step - 1].astype(jnp.float32)
    out_ref[...] = result

    def drain(h):
        for copy in own_copies(h) + relay_copies(h):
            copy.wait_send()
        for which in range(3):
            pair_copy(h, which).wait_send()
        for step in range(1, depth):
            q_copy(h, step).wait_send()
            o_copy(h, step).wait_send()
            stat_copy(h, step).wait_send()

    each_head(drain)
    for step in range(1, width):
        y_copy(step).wait_send()


def on_device(
    depth,
    width,
    queries,
    new_keys,
    new_values,
    key_cache,
    value_cache,
    out_weight,
    gate,
    refresh_index,
    refresh_count,
):
    slots, row_width = queries.shape
    tokens = key_cache.shape[0]
    heads = row_width // HD
    out_cols = gate.shape[0]
    groups = max(1, depth * slots // HD)
    bf16, f32 = jnp.bfloat16, jnp.float32
    dma = pltpu.SemaphoreType.DMA
    any_spec = pl.BlockSpec(memory_space=pl.ANY)
    vmem_spec = pl.BlockSpec(memory_space=pltpu.VMEM)
    projected = pl.pallas_call(
        functools.partial(kernel, (depth, width)),
        out_shape=jax.ShapeDtypeStruct((slots, out_cols), f32),
        in_specs=[any_spec] * 6 + [vmem_spec] * 2,
        out_specs=vmem_spec,
        scratch_shapes=[
            pltpu.VMEM((2, tokens, row_width), bf16),
            pltpu.VMEM((2, slots, row_width), bf16),
            pltpu.VMEM((heads, depth, slots, HD), bf16),
            pltpu.VMEM((heads, 2, X * CORES, tokens, HD), bf16),
            pltpu.VMEM((heads, depth, slots, HD), bf16),
            pltpu.VMEM((heads, depth, slots, HD), bf16),
            pltpu.VMEM((heads, groups, 2, 1, HD), f32),
            pltpu.VMEM((heads, depth, 2, 1, HD), f32),
            pltpu.VMEM(out_weight.shape, bf16),
            pltpu.VMEM((width, slots, out_cols), f32),
            pltpu.VMEM((max(1, width - 1), slots, out_cols), bf16),
            pltpu.VMEM((max(1, width - 1), slots, out_cols), bf16),
            dma((5 + heads,)),
            dma((heads, depth)),
            dma((heads, depth)),
            dma((heads, 2)),
            dma((heads, 2)),
            dma((heads, 2)),
            dma((heads, 2)),
            dma((heads, 3)),
            dma((heads, 3)),
            dma((heads, depth)),
            dma((heads, depth)),
            dma((heads, depth)),
            dma((heads, depth)),
            dma((max(1, width - 1),)),
            dma((max(1, width - 1),)),
        ],
        compiler_params=pltpu.CompilerParams(
            collective_id=0, has_side_effects=True, vmem_limit_bytes=67_043_328
        ),
    )(
        queries,
        new_keys,
        new_values,
        key_cache,
        value_cache,
        out_weight,
        refresh_index,
        refresh_count.reshape(1, 1),
    )
    live = lax.broadcasted_iota(jnp.int32, (slots, out_cols), 0) < refresh_count[0]
    return (gate[None] * jnp.where(live, projected, 0.0)).astype(bf16)


def solution(mesh):
    depth = mesh.shape["seq"] // (X * CORES)
    width = mesh.shape["head"]
    return jax.shard_map(
        functools.partial(on_device, depth, width),
        mesh=mesh,
        in_specs=(
            P("seq", "head"),
            P("seq", "head"),
            P("seq", "head"),
            P("seq", "head"),
            P("seq", "head"),
            P("head", None),
            P("head"),
            P("seq", None),
            P("seq"),
        ),
        out_specs=P("seq", "head"),
        check_vma=False,
    )
```

```python
import functools
import math

import jax
import jax.numpy as jnp
from jax import lax
from jax.experimental import pallas as pl
from jax.experimental.pallas import tpu as pltpu
from jax.sharding import PartitionSpec as P

HD = 128
X = 4
CORES = 2
MESH = pl.DeviceIdType.MESH
AHEAD = 3
LAG = 2


def kernel(
    rings,
    q_hbm,
    new_k_hbm,
    new_v_hbm,
    cache_k_hbm,
    cache_v_hbm,
    weight_hbm,
    index_ref,
    count_ref,
    out_ref,
    cache,
    fresh,
    q_buf,
    kv_buf,
    o_send,
    o_recv,
    stat_send,
    stat_recv,
    weight,
    proj,
    y_send,
    y_recv,
    local_sem,
    q_ssem,
    q_rsem,
    own_ssem,
    own_rsem,
    relay_ssem,
    relay_rsem,
    pair_ssem,
    pair_rsem,
    o_ssem,
    o_rsem,
    stat_ssem,
    stat_rsem,
    y_ssem,
    y_rsem,
    z_near,
    y_near,
):
    depth, width = rings
    heads = q_buf.shape[0]
    slots = q_buf.shape[2]
    tokens = kv_buf.shape[3]
    out_cols = out_ref.shape[1]
    groups = stat_send.shape[1]
    per_group = depth // groups
    factor = HD ** (-0.5) * math.log2(math.e)

    me = lax.axis_index("seq")
    y = lax.axis_index("head")
    z = me // (X * CORES)
    x = (me // CORES) % X
    core = me % CORES

    def at_seq(z_at, x_at, core_at):
        return {"seq": (z_at * X + x_at) * CORES + core_at, "head": y}

    def z_peer(step):
        return at_seq((z + step) % depth, x, core)

    def y_peer(step):
        return {"seq": me, "head": (y + step) % width}

    right = at_seq(z, (x + 1) % X, core)
    left = at_seq(z, (x + X - 1) % X, core)
    sibling = at_seq(z, x, 1 - core)

    def remote(src, dst, send, recv, device):
        return pltpu.make_async_remote_copy(
            src_ref=src,
            dst_ref=dst,
            send_sem=send,
            recv_sem=recv,
            device_id=device,
            device_id_type=MESH,
        )

    barrier = pltpu.get_barrier_semaphore()
    peers = (
        [z_peer(1), z_peer(depth - 1), y_peer(1), y_peer(width - 1)]
        + [right, left, sibling]
    )
    for peer in peers:
        pl.semaphore_signal(barrier, inc=1, device_id=peer, device_id_type=MESH)

    loads = [
        pltpu.make_async_copy(cache_k_hbm, cache.at[0], local_sem.at[0]),
        pltpu.make_async_copy(cache_v_hbm, cache.at[1], local_sem.at[1]),
        pltpu.make_async_copy(new_k_hbm, fresh.at[0], local_sem.at[2]),
        pltpu.make_async_copy(new_v_hbm, fresh.at[1], local_sem.at[3]),
    ]
    q_loads = [
        pltpu.make_async_copy(
            q_hbm.at[:, pl.ds(h * HD, HD)], q_buf.at[h, 0], local_sem.at[5 + h]
        )
        for h in range(heads)
    ]
    weight_load = pltpu.make_async_copy(weight_hbm, weight, local_sem.at[4])
    for load in loads + q_loads + [weight_load]:
        load.start()

    matches = (
        lax.broadcasted_iota(jnp.int32, (tokens, slots), 0) == index_ref[...]
    ) & (lax.broadcasted_iota(jnp.int32, (tokens, slots), 1) < count_ref[...])
    chosen = matches.astype(jnp.float32)
    replaced = jnp.max(chosen, axis=1, keepdims=True) > 0.5
    chosen = chosen.astype(jnp.bfloat16)
    for load in loads:
        load.wait()
    for part in range(2):
        placed = jnp.dot(chosen, fresh[part], preferred_element_type=jnp.float32)
        for h in range(heads):
            cols = slice(h * HD, (h + 1) * HD)
            kv_buf[h, part, 0] = jnp.where(
                replaced, placed[:, cols], cache[part, :, cols].astype(jnp.float32)
            ).astype(jnp.bfloat16)
    for load in q_loads:
        load.wait()

    pl.semaphore_wait(barrier, len(peers))

    def own_copies(h):
        src = kv_buf.at[h, :, 0]
        return (
            remote(src, kv_buf.at[h, :, 1], own_ssem.at[h, 0], own_rsem.at[h, 0], right),
            remote(src, kv_buf.at[h, :, 2], own_ssem.at[h, 1], own_rsem.at[h, 1], left),
        )

    def relay_copies(h):
        return (
            remote(
                kv_buf.at[h, 0, 1], kv_buf.at[h, 0, 3], relay_ssem.at[h, 0], relay_rsem.at[h, 0], right
            ),
            remote(
                kv_buf.at[h, 1, 2], kv_buf.at[h, 1, 3], relay_ssem.at[h, 1], relay_rsem.at[h, 1], left
            ),
        )

    def pair_copy(h, which):
        first, count = ((0, 1), (1, 2), (3, 1))[which]
        return remote(
            kv_buf.at[h, :, pl.ds(first, count)],
            kv_buf.at[h, :, pl.ds(X + first, count)],
            pair_ssem.at[h, which],
            pair_rsem.at[h, which],
            sibling,
        )

    def q_copy(h, step):
        return remote(
            q_buf.at[h, 0], q_buf.at[h, step], q_ssem.at[h, step], q_rsem.at[h, step], z_peer(step)
        )

    def o_copy(h, step):
        return remote(
            o_send.at[h, step],
            o_recv.at[h, step],
            o_ssem.at[h, step],
            o_rsem.at[h, step],
            z_peer(depth - step),
        )

    def stat_copy(h, step):
        return remote(
            stat_send.at[h, step // per_group],
            stat_recv.at[h, step],
            stat_ssem.at[h, step],
            stat_rsem.at[h, step],
            z_peer(depth - step),
        )

    far_first = sorted(range(1, depth), key=lambda step: -min(step, depth - step))

    def each_head(body):
        lax.fori_loop(0, heads, lambda h, carry: (body(h), carry)[1], 0)

    for h in range(min(AHEAD, heads)):
        for copy in own_copies(h):
            copy.start()
        pair_copy(h, 0).start()

    def send_queries(distance, h):
        for step in sorted({distance, depth - distance}):
            q_copy(h, step).start()

    def announce(sem, peer):
        pl.semaphore_signal(sem, inc=1, device_id=peer, device_id_type=MESH)

    announce(y_near, y_peer(1))
    for distance in range(1, depth // 2 + 1):
        if distance > 1:
            pl.semaphore_wait(z_near.at[0, distance - 1], 1)
            pl.semaphore_wait(z_near.at[1, distance - 1], 1)
        if distance < depth // 2:
            announce(z_near.at[0, distance], z_peer(1))
            announce(z_near.at[1, distance], z_peer(depth - 1))
        each_head(functools.partial(send_queries, distance))
    pl.semaphore_wait(y_near, 1)

    lane = lax.broadcasted_iota(jnp.int32, (per_group * slots, HD), 1)
    row = lax.broadcasted_iota(jnp.int32, (per_group * slots, HD), 0)
    diagonal = lane == row

    def to_row(column):
        spread = jnp.broadcast_to(column, (per_group * slots, HD))
        return jnp.sum(jnp.where(diagonal, spread, 0.0), axis=0, keepdims=True)

    def attend(h):
        queries = q_buf[h].reshape(depth * slots, HD)
        keys = kv_buf[h, 0].reshape(X * CORES * tokens, HD)
        values = kv_buf[h, 1].reshape(X * CORES * tokens, HD)
        scores = (
            lax.dot_general(
                queries, keys, (((1,), (1,)), ((), ())), preferred_element_type=jnp.float32
            )
            * factor
        )
        top = jnp.max(scores, axis=1, keepdims=True)
        weights = jnp.exp2(scores - top)
        total = jnp.sum(weights, axis=1, keepdims=True)
        summed = jnp.dot(
            weights.astype(jnp.bfloat16), values, preferred_element_type=jnp.float32
        ).astype(jnp.bfloat16)
        o_send[h] = summed.reshape(depth, slots, HD)
        o_recv[h, 0] = summed[:slots]
        for g in range(groups):
            rows = slice(g * per_group * slots, (g + 1) * per_group * slots)
            top_row, total_row = to_row(top[rows]), to_row(total[rows])
            stat_send[h, g, 0] = top_row
            stat_send[h, g, 1] = total_row
            if g == 0:
                stat_recv[h, 0, 0] = top_row
                stat_recv[h, 0, 1] = total_row

    def stage(step, carry):
        @pl.when(step < heads)
        def _():
            for copy in own_copies(step):
                copy.wait_recv()
            for copy in relay_copies(step):
                copy.start()
            pair_copy(step, 1).start()

            @pl.when(step + AHEAD < heads)
            def _():
                for copy in own_copies(step + AHEAD):
                    copy.start()
                pair_copy(step + AHEAD, 0).start()

        @pl.when((step >= 1) & (step <= heads))
        def _():
            h = step - 1
            for copy in relay_copies(h):
                copy.wait_recv()
            pair_copy(h, 2).start()

        @pl.when(step >= LAG)
        def _():
            h = step - LAG
            for ring in range(1, depth):
                q_copy(h, ring).wait_recv()
            for which in range(3):
                pair_copy(h, which).wait_recv()
            attend(h)
            for ring in far_first:
                o_copy(h, ring).start()
                stat_copy(h, ring).start()

        return carry

    lax.fori_loop(0, heads + LAG, stage, 0)

    weight_load.wait()
    lane_row = lax.broadcasted_iota(jnp.int32, (1, HD), 1) // slots
    lanes = depth * slots
    spot = lax.broadcasted_iota(jnp.int32, (slots, lanes), 1) % slots
    on_row = spot == lax.broadcasted_iota(jnp.int32, (slots, lanes), 0)

    def over_lanes(rows, op):
        folded = functools.reduce(op, rows)
        shift = slots
        while shift < HD:
            folded = op(folded, pltpu.roll(folded, shift, 1))
            shift *= 2
        return folded

    def combined(h):
        for step in range(1, depth):
            o_copy(h, step).wait_recv()
            stat_copy(h, step).wait_recv()
        tops, totals = [], []
        for g in range(groups):
            top_row, total_row = (stat_recv[h, g * per_group, 0], stat_recv[h, g * per_group, 1])
            for k in range(1, per_group):
                here = lane_row == k
                top_row = jnp.where(here, stat_recv[h, g * per_group + k, 0], top_row)
                total_row = jnp.where(here, stat_recv[h, g * per_group + k, 1], total_row)
            tops.append(top_row)
            totals.append(total_row)
        peak = over_lanes(tops, jnp.maximum)
        shares = [jnp.exp2(top_row - peak) for top_row in tops]
        whole = over_lanes([share * total for share, total in zip(shares, totals)], jnp.add)
        factors = jnp.concatenate([share / whole for share in shares], axis=1)
        spread = jnp.where(on_row, jnp.broadcast_to(factors, (slots, lanes)), 0.0)
        high = spread.astype(jnp.bfloat16)
        low = (spread - high.astype(jnp.float32)).astype(jnp.bfloat16)
        parts = o_recv[h].reshape(lanes, HD)
        return (
            jnp.dot(high, parts, preferred_element_type=jnp.float32)
            + jnp.dot(low, parts, preferred_element_type=jnp.float32)
        ).astype(jnp.bfloat16)

    def projected(attended, h, step):
        start = pl.multiple_of(((y + step) % width) * out_cols, HD)
        block = weight[pl.ds(pl.multiple_of(h * HD, HD), HD), pl.ds(start, out_cols)]
        return jnp.dot(attended, block, preferred_element_type=jnp.float32)

    proj[...] = jnp.zeros_like(proj)

    def project(h, carry):
        attended = combined(h)
        for step in range(width):
            proj[step] += projected(attended, h, step)
        return carry

    lax.fori_loop(0, heads - 1, project, 0)

    def y_copy(step):
        return remote(
            y_send.at[step - 1], y_recv.at[step - 1], y_ssem.at[step - 1], y_rsem.at[step - 1], y_peer(step)
        )

    attended = combined(heads - 1)
    for step in sorted(range(1, width), key=lambda step: -min(step, width - step)):
        y_send[step - 1] = (proj[step] + projected(attended, heads - 1, step)).astype(jnp.bfloat16)
        y_copy(step).start()
    result = proj[0] + projected(attended, heads - 1, 0)
    for step in range(1, width):
        y_copy(step).wait_recv()
        result += y_recv[step - 1].astype(jnp.float32)
    out_ref[...] = result

    def drain(h):
        for copy in own_copies(h) + relay_copies(h):
            copy.wait_send()
        for which in range(3):
            pair_copy(h, which).wait_send()
        for step in range(1, depth):
            q_copy(h, step).wait_send()
            o_copy(h, step).wait_send()
            stat_copy(h, step).wait_send()

    each_head(drain)
    for step in range(1, width):
        y_copy(step).wait_send()


def on_device(
    depth,
    width,
    queries,
    new_keys,
    new_values,
    key_cache,
    value_cache,
    out_weight,
    gate,
    refresh_index,
    refresh_count,
):
    slots, row_width = queries.shape
    tokens = key_cache.shape[0]
    heads = row_width // HD
    out_cols = gate.shape[0]
    groups = max(1, depth * slots // HD)
    bf16, f32 = jnp.bfloat16, jnp.float32
    dma = pltpu.SemaphoreType.DMA
    any_spec = pl.BlockSpec(memory_space=pl.ANY)
    vmem_spec = pl.BlockSpec(memory_space=pltpu.VMEM)
    projected = pl.pallas_call(
        functools.partial(kernel, (depth, width)),
        out_shape=jax.ShapeDtypeStruct((slots, out_cols), f32),
        in_specs=[any_spec] * 6 + [vmem_spec] * 2,
        out_specs=vmem_spec,
        scratch_shapes=[
            pltpu.VMEM((2, tokens, row_width), bf16),
            pltpu.VMEM((2, slots, row_width), bf16),
            pltpu.VMEM((heads, depth, slots, HD), bf16),
            pltpu.VMEM((heads, 2, X * CORES, tokens, HD), bf16),
            pltpu.VMEM((heads, depth, slots, HD), bf16),
            pltpu.VMEM((heads, depth, slots, HD), bf16),
            pltpu.VMEM((heads, groups, 2, 1, HD), f32),
            pltpu.VMEM((heads, depth, 2, 1, HD), f32),
            pltpu.VMEM(out_weight.shape, bf16),
            pltpu.VMEM((width, slots, out_cols), f32),
            pltpu.VMEM((max(1, width - 1), slots, out_cols), bf16),
            pltpu.VMEM((max(1, width - 1), slots, out_cols), bf16),
            dma((5 + heads,)),
            dma((heads, depth)),
            dma((heads, depth)),
            dma((heads, 2)),
            dma((heads, 2)),
            dma((heads, 2)),
            dma((heads, 2)),
            dma((heads, 3)),
            dma((heads, 3)),
            dma((heads, depth)),
            dma((heads, depth)),
            dma((heads, depth)),
            dma((heads, depth)),
            dma((max(1, width - 1),)),
            dma((max(1, width - 1),)),
            pltpu.SemaphoreType.REGULAR((2, max(2, depth // 2))),
            pltpu.SemaphoreType.REGULAR,
        ],
        compiler_params=pltpu.CompilerParams(
            collective_id=0, has_side_effects=True, vmem_limit_bytes=67_043_328
        ),
    )(
        queries,
        new_keys,
        new_values,
        key_cache,
        value_cache,
        out_weight,
        refresh_index,
        refresh_count.reshape(1, 1),
    )
    live = lax.broadcasted_iota(jnp.int32, (slots, out_cols), 0) < refresh_count[0]
    return (gate[None] * jnp.where(live, projected, 0.0)).astype(bf16)


def solution(mesh):
    depth = mesh.shape["seq"] // (X * CORES)
    width = mesh.shape["head"]
    return jax.shard_map(
        functools.partial(on_device, depth, width),
        mesh=mesh,
        in_specs=(
            P("seq", "head"),
            P("seq", "head"),
            P("seq", "head"),
            P("seq", "head"),
            P("seq", "head"),
            P("head", None),
            P("head"),
            P("seq", None),
            P("seq"),
        ),
        out_specs=P("seq", "head"),
        check_vma=False,
    )
```

```python
import functools
import math

import jax
import jax.numpy as jnp
from jax import lax
from jax.experimental import pallas as pl
from jax.experimental.pallas import tpu as pltpu
from jax.sharding import PartitionSpec as P

HD = 128
X = 4
CORES = 2
MESH = pl.DeviceIdType.MESH
AHEAD = 3
LAG = 2


def kernel(
    rings,
    q_hbm,
    new_k_hbm,
    new_v_hbm,
    cache_k_hbm,
    cache_v_hbm,
    weight_hbm,
    index_ref,
    count_ref,
    out_ref,
    cache,
    fresh,
    q_buf,
    kv_buf,
    o_send,
    o_recv,
    stat_send,
    stat_recv,
    weight,
    proj,
    y_send,
    y_recv,
    local_sem,
    q_ssem,
    q_rsem,
    own_ssem,
    own_rsem,
    relay_ssem,
    relay_rsem,
    pair_ssem,
    pair_rsem,
    o_ssem,
    o_rsem,
    stat_ssem,
    stat_rsem,
    y_ssem,
    y_rsem,
    z_near,
    y_near,
):
    depth, width = rings
    heads = q_buf.shape[0]
    slots = q_buf.shape[2]
    tokens = kv_buf.shape[3]
    out_cols = out_ref.shape[1]
    groups = stat_send.shape[1]
    per_group = depth // groups
    factor = HD ** (-0.5) * math.log2(math.e)

    me = lax.axis_index("seq")
    y = lax.axis_index("head")
    z = me // (X * CORES)
    x = (me // CORES) % X
    core = me % CORES

    def at_seq(z_at, x_at, core_at):
        return {"seq": (z_at * X + x_at) * CORES + core_at, "head": y}

    def z_peer(step):
        return at_seq((z + step) % depth, x, core)

    def y_peer(step):
        return {"seq": me, "head": (y + step) % width}

    right = at_seq(z, (x + 1) % X, core)
    left = at_seq(z, (x + X - 1) % X, core)
    sibling = at_seq(z, x, 1 - core)

    def remote(src, dst, send, recv, device):
        return pltpu.make_async_remote_copy(
            src_ref=src,
            dst_ref=dst,
            send_sem=send,
            recv_sem=recv,
            device_id=device,
            device_id_type=MESH,
        )

    barrier = pltpu.get_barrier_semaphore()
    peers = (
        [z_peer(1), z_peer(depth - 1), y_peer(1), y_peer(width - 1)]
        + [right, left, sibling]
    )
    for peer in peers:
        pl.semaphore_signal(barrier, inc=1, device_id=peer, device_id_type=MESH)

    loads = [
        pltpu.make_async_copy(cache_k_hbm, cache.at[0], local_sem.at[0]),
        pltpu.make_async_copy(cache_v_hbm, cache.at[1], local_sem.at[1]),
        pltpu.make_async_copy(new_k_hbm, fresh.at[0], local_sem.at[2]),
        pltpu.make_async_copy(new_v_hbm, fresh.at[1], local_sem.at[3]),
    ]
    q_loads = [
        pltpu.make_async_copy(
            q_hbm.at[:, pl.ds(h * HD, HD)], q_buf.at[h, 0], local_sem.at[5 + h]
        )
        for h in range(heads)
    ]
    weight_load = pltpu.make_async_copy(weight_hbm, weight, local_sem.at[4])
    for load in loads + q_loads:
        load.start()

    matches = (
        lax.broadcasted_iota(jnp.int32, (tokens, slots), 0) == index_ref[...]
    ) & (lax.broadcasted_iota(jnp.int32, (tokens, slots), 1) < count_ref[...])
    chosen = matches.astype(jnp.float32)
    replaced = jnp.max(chosen, axis=1, keepdims=True) > 0.5
    chosen = chosen.astype(jnp.bfloat16)
    for load in loads:
        load.wait()
    for part in range(2):
        placed = jnp.dot(chosen, fresh[part], preferred_element_type=jnp.float32)
        for h in range(heads):
            cols = slice(h * HD, (h + 1) * HD)
            kv_buf[h, part, 0] = jnp.where(
                replaced, placed[:, cols], cache[part, :, cols].astype(jnp.float32)
            ).astype(jnp.bfloat16)
    pl.semaphore_wait(barrier, len(peers))

    def own_copies(h):
        src = kv_buf.at[h, :, 0]
        return (
            remote(src, kv_buf.at[h, :, 1], own_ssem.at[h, 0], own_rsem.at[h, 0], right),
            remote(src, kv_buf.at[h, :, 2], own_ssem.at[h, 1], own_rsem.at[h, 1], left),
        )

    def relay_copies(h):
        return (
            remote(
                kv_buf.at[h, 0, 1], kv_buf.at[h, 0, 3], relay_ssem.at[h, 0], relay_rsem.at[h, 0], right
            ),
            remote(
                kv_buf.at[h, 1, 2], kv_buf.at[h, 1, 3], relay_ssem.at[h, 1], relay_rsem.at[h, 1], left
            ),
        )

    def pair_copy(h, which):
        first, count = ((0, 1), (1, 2), (3, 1))[which]
        return remote(
            kv_buf.at[h, :, pl.ds(first, count)],
            kv_buf.at[h, :, pl.ds(X + first, count)],
            pair_ssem.at[h, which],
            pair_rsem.at[h, which],
            sibling,
        )

    def q_copy(h, step):
        return remote(
            q_buf.at[h, 0], q_buf.at[h, step], q_ssem.at[h, step], q_rsem.at[h, step], z_peer(step)
        )

    def o_copy(h, step):
        return remote(
            o_send.at[h, step],
            o_recv.at[h, step],
            o_ssem.at[h, step],
            o_rsem.at[h, step],
            z_peer(depth - step),
        )

    def stat_copy(h, step):
        return remote(
            stat_send.at[h, step // per_group],
            stat_recv.at[h, step],
            stat_ssem.at[h, step],
            stat_rsem.at[h, step],
            z_peer(depth - step),
        )

    far_first = sorted(range(1, depth), key=lambda step: -min(step, depth - step))

    def each_head(body):
        lax.fori_loop(0, heads, lambda h, carry: (body(h), carry)[1], 0)

    for h in range(min(AHEAD, heads)):
        for copy in own_copies(h):
            copy.start()
        pair_copy(h, 0).start()
    weight_load.start()
    for load in q_loads:
        load.wait()

    def send_queries(distance, h):
        for step in sorted({distance, depth - distance}):
            q_copy(h, step).start()

    def announce(sem, peer):
        pl.semaphore_signal(sem, inc=1, device_id=peer, device_id_type=MESH)

    announce(y_near, y_peer(1))
    for distance in range(1, depth // 2 + 1):
        if distance > 1:
            pl.semaphore_wait(z_near.at[0, distance - 1], 1)
            pl.semaphore_wait(z_near.at[1, distance - 1], 1)
        if distance < depth // 2:
            announce(z_near.at[0, distance], z_peer(1))
            announce(z_near.at[1, distance], z_peer(depth - 1))
        each_head(functools.partial(send_queries, distance))
    pl.semaphore_wait(y_near, 1)

    lane = lax.broadcasted_iota(jnp.int32, (per_group * slots, HD), 1)
    row = lax.broadcasted_iota(jnp.int32, (per_group * slots, HD), 0)
    diagonal = lane == row

    def to_row(column):
        spread = jnp.broadcast_to(column, (per_group * slots, HD))
        return jnp.sum(jnp.where(diagonal, spread, 0.0), axis=0, keepdims=True)

    def attend(h):
        queries = q_buf[h].reshape(depth * slots, HD)
        keys = kv_buf[h, 0].reshape(X * CORES * tokens, HD)
        values = kv_buf[h, 1].reshape(X * CORES * tokens, HD)
        scores = (
            lax.dot_general(
                queries, keys, (((1,), (1,)), ((), ())), preferred_element_type=jnp.float32
            )
            * factor
        )
        top = jnp.max(scores, axis=1, keepdims=True)
        weights = jnp.exp2(scores - top)
        total = jnp.sum(weights, axis=1, keepdims=True)
        summed = jnp.dot(
            weights.astype(jnp.bfloat16), values, preferred_element_type=jnp.float32
        ).astype(jnp.bfloat16)
        o_send[h] = summed.reshape(depth, slots, HD)
        o_recv[h, 0] = summed[:slots]
        for g in range(groups):
            rows = slice(g * per_group * slots, (g + 1) * per_group * slots)
            top_row, total_row = to_row(top[rows]), to_row(total[rows])
            stat_send[h, g, 0] = top_row
            stat_send[h, g, 1] = total_row
            if g == 0:
                stat_recv[h, 0, 0] = top_row
                stat_recv[h, 0, 1] = total_row

    def stage(step, carry):
        @pl.when(step < heads)
        def _():
            for copy in own_copies(step):
                copy.wait_recv()
            for copy in relay_copies(step):
                copy.start()
            pair_copy(step, 1).start()

            @pl.when(step + AHEAD < heads)
            def _():
                for copy in own_copies(step + AHEAD):
                    copy.start()
                pair_copy(step + AHEAD, 0).start()

        @pl.when((step >= 1) & (step <= heads))
        def _():
            h = step - 1
            for copy in relay_copies(h):
                copy.wait_recv()
            pair_copy(h, 2).start()

        @pl.when(step >= LAG)
        def _():
            h = step - LAG
            for ring in range(1, depth):
                q_copy(h, ring).wait_recv()
            for which in range(3):
                pair_copy(h, which).wait_recv()
            attend(h)
            for ring in far_first:
                o_copy(h, ring).start()
                stat_copy(h, ring).start()

        return carry

    lax.fori_loop(0, heads + LAG, stage, 0)

    weight_load.wait()
    lane_row = lax.broadcasted_iota(jnp.int32, (1, HD), 1) // slots
    lanes = depth * slots
    spot = lax.broadcasted_iota(jnp.int32, (slots, lanes), 1) % slots
    on_row = spot == lax.broadcasted_iota(jnp.int32, (slots, lanes), 0)

    def over_lanes(rows, op):
        folded = functools.reduce(op, rows)
        shift = slots
        while shift < HD:
            folded = op(folded, pltpu.roll(folded, shift, 1))
            shift *= 2
        return folded

    def combined(h):
        for step in range(1, depth):
            o_copy(h, step).wait_recv()
            stat_copy(h, step).wait_recv()
        tops, totals = [], []
        for g in range(groups):
            top_row, total_row = (stat_recv[h, g * per_group, 0], stat_recv[h, g * per_group, 1])
            for k in range(1, per_group):
                here = lane_row == k
                top_row = jnp.where(here, stat_recv[h, g * per_group + k, 0], top_row)
                total_row = jnp.where(here, stat_recv[h, g * per_group + k, 1], total_row)
            tops.append(top_row)
            totals.append(total_row)
        peak = over_lanes(tops, jnp.maximum)
        shares = [jnp.exp2(top_row - peak) for top_row in tops]
        whole = over_lanes([share * total for share, total in zip(shares, totals)], jnp.add)
        factors = jnp.concatenate([share / whole for share in shares], axis=1)
        spread = jnp.where(on_row, jnp.broadcast_to(factors, (slots, lanes)), 0.0)
        high = spread.astype(jnp.bfloat16)
        low = (spread - high.astype(jnp.float32)).astype(jnp.bfloat16)
        parts = o_recv[h].reshape(lanes, HD)
        return (
            jnp.dot(high, parts, preferred_element_type=jnp.float32)
            + jnp.dot(low, parts, preferred_element_type=jnp.float32)
        ).astype(jnp.bfloat16)

    def projected(attended, h, step):
        start = pl.multiple_of(((y + step) % width) * out_cols, HD)
        block = weight[pl.ds(pl.multiple_of(h * HD, HD), HD), pl.ds(start, out_cols)]
        return jnp.dot(attended, block, preferred_element_type=jnp.float32)

    proj[...] = jnp.zeros_like(proj)

    def project(h, carry):
        attended = combined(h)
        for step in range(width):
            proj[step] += projected(attended, h, step)
        return carry

    lax.fori_loop(0, heads - 1, project, 0)

    def y_copy(step):
        return remote(
            y_send.at[step - 1], y_recv.at[step - 1], y_ssem.at[step - 1], y_rsem.at[step - 1], y_peer(step)
        )

    attended = combined(heads - 1)
    for step in sorted(range(1, width), key=lambda step: -min(step, width - step)):
        y_send[step - 1] = (proj[step] + projected(attended, heads - 1, step)).astype(jnp.bfloat16)
        y_copy(step).start()
    result = proj[0] + projected(attended, heads - 1, 0)
    for step in range(1, width):
        y_copy(step).wait_recv()
        result += y_recv[step - 1].astype(jnp.float32)
    out_ref[...] = result

    def drain(h):
        for copy in own_copies(h) + relay_copies(h):
            copy.wait_send()
        for which in range(3):
            pair_copy(h, which).wait_send()
        for step in range(1, depth):
            q_copy(h, step).wait_send()
            o_copy(h, step).wait_send()
            stat_copy(h, step).wait_send()

    each_head(drain)
    for step in range(1, width):
        y_copy(step).wait_send()


def on_device(
    depth,
    width,
    queries,
    new_keys,
    new_values,
    key_cache,
    value_cache,
    out_weight,
    gate,
    refresh_index,
    refresh_count,
):
    slots, row_width = queries.shape
    tokens = key_cache.shape[0]
    heads = row_width // HD
    out_cols = gate.shape[0]
    groups = max(1, depth * slots // HD)
    bf16, f32 = jnp.bfloat16, jnp.float32
    dma = pltpu.SemaphoreType.DMA
    any_spec = pl.BlockSpec(memory_space=pl.ANY)
    vmem_spec = pl.BlockSpec(memory_space=pltpu.VMEM)
    projected = pl.pallas_call(
        functools.partial(kernel, (depth, width)),
        out_shape=jax.ShapeDtypeStruct((slots, out_cols), f32),
        in_specs=[any_spec] * 6 + [vmem_spec] * 2,
        out_specs=vmem_spec,
        scratch_shapes=[
            pltpu.VMEM((2, tokens, row_width), bf16),
            pltpu.VMEM((2, slots, row_width), bf16),
            pltpu.VMEM((heads, depth, slots, HD), bf16),
            pltpu.VMEM((heads, 2, X * CORES, tokens, HD), bf16),
            pltpu.VMEM((heads, depth, slots, HD), bf16),
            pltpu.VMEM((heads, depth, slots, HD), bf16),
            pltpu.VMEM((heads, groups, 2, 1, HD), f32),
            pltpu.VMEM((heads, depth, 2, 1, HD), f32),
            pltpu.VMEM(out_weight.shape, bf16),
            pltpu.VMEM((width, slots, out_cols), f32),
            pltpu.VMEM((max(1, width - 1), slots, out_cols), bf16),
            pltpu.VMEM((max(1, width - 1), slots, out_cols), bf16),
            dma((5 + heads,)),
            dma((heads, depth)),
            dma((heads, depth)),
            dma((heads, 2)),
            dma((heads, 2)),
            dma((heads, 2)),
            dma((heads, 2)),
            dma((heads, 3)),
            dma((heads, 3)),
            dma((heads, depth)),
            dma((heads, depth)),
            dma((heads, depth)),
            dma((heads, depth)),
            dma((max(1, width - 1),)),
            dma((max(1, width - 1),)),
            pltpu.SemaphoreType.REGULAR((2, max(2, depth // 2))),
            pltpu.SemaphoreType.REGULAR,
        ],
        compiler_params=pltpu.CompilerParams(
            collective_id=0, has_side_effects=True, vmem_limit_bytes=67_043_328
        ),
    )(
        queries,
        new_keys,
        new_values,
        key_cache,
        value_cache,
        out_weight,
        refresh_index,
        refresh_count.reshape(1, 1),
    )
    live = lax.broadcasted_iota(jnp.int32, (slots, out_cols), 0) < refresh_count[0]
    return (gate[None] * jnp.where(live, projected, 0.0)).astype(bf16)


def solution(mesh):
    depth = mesh.shape["seq"] // (X * CORES)
    width = mesh.shape["head"]
    return jax.shard_map(
        functools.partial(on_device, depth, width),
        mesh=mesh,
        in_specs=(
            P("seq", "head"),
            P("seq", "head"),
            P("seq", "head"),
            P("seq", "head"),
            P("seq", "head"),
            P("head", None),
            P("head"),
            P("seq", None),
            P("seq"),
        ),
        out_specs=P("seq", "head"),
        check_vma=False,
    )
```
